32 devices in a mesh: row: 4 (over x, core), col: 8 (over z, y).
Axes of the slice: x: 2, y: 2, z: 4, core: 2. Of those that a mesh axis runs over, the one named last changes fastest.
Arguments:
- panel: bfloat16 [3072, 98304], P('row', 'col'), may hold values from -0.01953125 to 0.01953125
- surface: bfloat16 [98304, 1024], P('col'), may hold values from -6 to 6
- flexibility: float32 [4, 768, 768], P('row'), may hold values from -0.21875 to 0.21875
- owner_map: int32 [24], replicated, may hold values from 0 to 23, each once
- adjacency: int32 [4, 2], P('row'), may hold values from 0 to 3, as said below
- live_rows: int32 [24], replicated, may hold values from 1 to 128, 2304 in all
Outputs:
- response: float32 [1024, 98304], P('row', 'col')
The draws below stay inside these ranges and needn't reach their ends.
Inputs may be any that keep to these rules, and one draw needn't show every extreme that they name: `adjacency`: each substructure lists 2 different neighbours, never itself. `owner_map`: every slot receives exactly one mortar block. `live_rows`: the live rows add up to 2304 and some block is full.
All inputs are finite; a program needn't handle non-finite values.
Results may differ from the reference program's by a relative error of at most 0.0029.
Values may be sent and summed in bfloat16 or wider, within the bound.
A program may use at most 192 MiB of HBM per device.

```python
import math
import jax
import jax.numpy as jnp
import numpy as np
from jax import lax

ORDER = 768
MBLK = 128
NC = 98304
L = 1024
ITERS = 2
DEG = 2
NSUB = 4
M = 3072
NBLK = 24
N_ROW = 4


def draw_adjacency(key, part):
    first_key, second_key = jax.random.split(jax.random.fold_in(key, 11))
    first_step = jax.random.randint(first_key, (NSUB,), 1, NSUB)
    second_step = jax.random.randint(second_key, (NSUB,), 1, NSUB - 1)
    second_step = jnp.where(second_step >= first_step, second_step + 1, second_step)
    own_index = jnp.arange(NSUB, dtype=jnp.int32)
    return jnp.stack([(own_index + first_step) % NSUB, (own_index + second_step) % NSUB], axis=1).astype(jnp.int32)


def block_scale(stream_key, shape, pieces, low, high):
    factor_of, own = 1.0, jax.random.fold_in(stream_key, 6)
    for axis_at, blocks in pieces:
        heights = jnp.exp(jax.random.uniform(jax.random.fold_in(own, axis_at), (blocks,), jnp.float32, low / len(pieces), high / len(pieces)))
        factor_of = factor_of * jnp.repeat(heights, shape[axis_at] // blocks).reshape([-1 if axis == axis_at else 1 for axis in range(len(shape))])
    return factor_of


def split_up(number_of, total, reach, slope):
    portions = [(1 << 20) // math.isqrt(rank ** slope) + 1 for rank in range(2, number_of + 1)]
    rest, given = total - reach - (number_of - 1), [1] * (number_of - 1)
    while rest > 0:
        movable = [i for i in range(number_of - 1) if given[i] < reach]
        mass, remaining = sum([portions[i] for i in movable]), rest
        for i in movable:
            more = min(reach - given[i], max(1, remaining * portions[i] // mass), rest)
            given[i] = given[i] + more
            rest = rest - more
    return np.array([reach] + given)


def ragged(key, number_of, total, most, slope):
    if number_of == 2:
        one = jax.random.randint(key, (), max(1, total - most), min(most, total - 1) + 1)
        return jnp.stack([one, total - one])
    lengths = jnp.asarray(split_up(number_of, total, most, slope), jnp.int32)
    pairs = (number_of - 1) // 2
    donor, taker = lengths[1:1 + 2 * pairs:2], lengths[2:2 + 2 * pairs:2]
    room = jnp.minimum(donor - 1, most - taker)
    shifted = jax.random.randint(jax.random.fold_in(key, 1), (pairs,), 0, 1 << 20) % (room + 1)
    lengths = lengths.at[1:1 + 2 * pairs:2].set(donor - shifted).at[2:2 + 2 * pairs:2].set(taker + shifted)
    return lengths[jax.random.permutation(jax.random.fold_in(key, 2), number_of)]


def gaussian(rng, extent, width, bound, pieces=(), kind=jnp.bfloat16):
    drawn = width * jax.random.normal(rng, extent, jnp.float32)
    if pieces:
        drawn = drawn * block_scale(rng, extent, pieces, -0.22, 0.18)
    return jnp.clip(drawn, -bound, bound).astype(kind)


def setup_inputs(seed: int = 0) -> dict:
    splits = jax.random.split(jax.random.key(seed), 7)
    panel = gaussian(splits[0], (M, NC), NC ** -0.5, 0.01953125, ((0, 4), (1, 8)))
    surface = gaussian(splits[1], (NC, L), 1.0, 6.0, ((0, 8),))
    flexibility = gaussian(splits[2], (NSUB, ORDER, ORDER), ORDER ** -0.5, 0.21875, ((0, 4),), jnp.float32)
    owner_map = jax.random.permutation(splits[3], NBLK).astype(jnp.int32)
    adjacency = draw_adjacency(jax.random.fold_in(splits[6], 71), 0)
    live_rows = ragged(splits[5], NBLK, NBLK * 3 * MBLK // 4, MBLK, 2).astype(jnp.int32)
    return dict(panel=panel, surface=surface, flexibility=flexibility, owner_map=owner_map, adjacency=adjacency, live_rows=live_rows)


DAMPING = 0.6
COUPLING = 0.5

def live_pattern(live_rows):
    offsets = jnp.arange(MBLK, dtype=jnp.int32)
    return (offsets[None, :] < live_rows[:, None]).astype(jnp.float32)

def reference(panel, surface, flexibility, owner_map, adjacency, live_rows):
    traction = lax.dot_general(surface, panel, (((0,), (1,)), ((), ())), preferred_element_type=jnp.float32)
    pattern = live_pattern(live_rows)
    blocks = traction.reshape(L, NBLK, MBLK) * pattern[None]
    inverse = jnp.zeros((NBLK,), jnp.int32).at[owner_map].set(jnp.arange(NBLK, dtype=jnp.int32))
    load_blocks = jnp.take(blocks, inverse, axis=1).reshape(L, NSUB, ORDER)
    neighbour_matrix = jnp.zeros((NSUB, NSUB), jnp.float32)
    for column in range(DEG):
        hits = adjacency[:, column][:, None] == jnp.arange(NSUB, dtype=jnp.int32)[None, :]
        neighbour_matrix = neighbour_matrix + hits.astype(jnp.float32)
    traces = jnp.zeros((L, NSUB, ORDER), jnp.float32)
    for sweep_index in range(ITERS):
        coupled = load_blocks + COUPLING * jnp.einsum('sn,lno->lso', neighbour_matrix, traces, precision=lax.Precision.HIGHEST)
        applied = jnp.einsum('sij,lsj->lsi', flexibility, coupled, precision=lax.Precision.HIGHEST)
        traces = (1.0 - DAMPING) * traces + DAMPING * applied
    rounded = traces.astype(jnp.bfloat16).reshape(L, NBLK, MBLK)
    updated = (jnp.take(rounded, owner_map, axis=1) * pattern[None].astype(jnp.bfloat16)).reshape(L, M)
    gain_factor = math.sqrt(NC / M)
    running_total = jnp.zeros((L, NC), jnp.float32)
    for block_row in range(N_ROW):
        lower = block_row * ORDER
        row_term = gain_factor * jnp.dot(updated[:, lower:lower + ORDER], panel[lower:lower + ORDER, :], preferred_element_type=jnp.float32)
        running_total = running_total + row_term
    return running_total
```

```python
import functools
import math

import jax
import jax.numpy as jnp
from jax import lax
from jax.experimental import pallas as pl
from jax.experimental.pallas import tpu as pltpu
from jax.sharding import PartitionSpec as P

MBLK = 128
ITERS = 2
DAMPING = 0.6
COUPLING = 0.5
TILE = 512
GATHERED_SIXTEENTHS = 8
PIECES = 3


def live_pattern(live_rows):
    offsets = jnp.arange(MBLK, dtype=jnp.int32)
    return (offsets[None, :] < live_rows[:, None]).astype(jnp.float32)


def product_kernel(count, gain, with_extra, with_base, *refs):
    factors, panels = refs[:count], refs[count : 2 * count]
    rest = refs[2 * count :]
    total = jnp.dot(factors[0][...], panels[0][...], preferred_element_type=jnp.float32)
    for factor, panel in zip(factors[1:], panels[1:]):
        total += jnp.dot(factor[...], panel[...], preferred_element_type=jnp.float32)
    total = gain * total
    if with_extra:
        total += rest[0][...].astype(jnp.float32)
    rest[-1][...] = total.astype(rest[-1].dtype)


def product(factors, panels, gain, columns, out_shape, out_start=0, extra=None, base=None):
    starts, width = columns
    count = len(factors)
    rows, depth = factors[0].shape
    in_specs = [pl.BlockSpec(f.shape, lambda j: (0, 0)) for f in factors]
    for start in starts:
        in_specs.append(
            pl.BlockSpec((depth, TILE), functools.partial(lambda s, j: (0, s + j), start // TILE))
        )
    operands = list(factors) + list(panels)
    if extra is not None:
        in_specs.append(pl.BlockSpec((rows, TILE), lambda j: (0, j)))
        operands.append(extra)
    aliases = {}
    if base is not None:
        in_specs.append(pl.BlockSpec(memory_space=pl.ANY))
        aliases = {len(operands): 0}
        operands.append(base)
    return pl.pallas_call(
        functools.partial(product_kernel, count, gain, extra is not None, base is not None),
        grid=(width // TILE,),
        in_specs=in_specs,
        out_specs=pl.BlockSpec(
            (rows, TILE), functools.partial(lambda s, j: (0, s + j), out_start // TILE)
        ),
        out_shape=out_shape,
        input_output_aliases=aliases,
        compiler_params=pltpu.CompilerParams(
            dimension_semantics=("arbitrary",), vmem_limit_bytes=40 * 1024 * 1024
        ),
        cost_estimate=pl.CostEstimate(
            flops=2 * rows * depth * count * width,
            bytes_accessed=2 * depth * count * width + 4 * rows * width,
            transcendentals=0,
        ),
    )(*operands)


def body(panel, surface, flexibility, owner_map, adjacency, live_rows):
    order_rows, column_count = panel.shape
    row_total = lax.axis_size("row")
    col_total = lax.axis_size("col")
    own_row = lax.axis_index("row")
    load_total = surface.shape[1]
    load_share = load_total // col_total
    group = load_total // row_total
    block_count = order_rows // MBLK
    swap = [(i, i ^ 1) for i in range(row_total)]
    across = [(i, i ^ 2) for i in range(row_total)]

    gathered = max(TILE, column_count * GATHERED_SIXTEENTHS // 16 // TILE * TILE)
    far = lax.ppermute(panel[:, :gathered], "row", across)
    partner = lax.ppermute(panel, "row", swap)
    far_partner = lax.ppermute(far, "row", swap)

    partial = lax.dot_general(
        surface, panel, (((0,), (1,)), ((), ())), preferred_element_type=jnp.float32
    )
    traction = lax.psum_scatter(
        partial.reshape(row_total, group, order_rows), "col", scatter_dimension=1, tiled=True
    )
    pattern = live_pattern(live_rows)
    own_pattern = lax.dynamic_slice_in_dim(pattern, own_row * block_count, block_count, 0)
    blocks = traction.reshape(load_share, block_count, MBLK) * own_pattern[None]
    every_block = lax.all_gather(blocks, "row", axis=1, tiled=True)
    block_total = owner_map.shape[0]
    inverse = (
        jnp.zeros((block_total,), jnp.int32)
        .at[owner_map]
        .set(jnp.arange(block_total, dtype=jnp.int32))
    )
    own_sources = lax.dynamic_slice_in_dim(inverse, own_row * block_count, block_count, 0)
    load_blocks = jnp.take(every_block, own_sources, axis=1).reshape(load_share, order_rows)
    hits = adjacency[0][:, None] == jnp.arange(row_total, dtype=jnp.int32)[None, :]
    neighbour_weights = jnp.sum(hits.astype(jnp.float32), axis=0)
    flex_local = flexibility[0]
    traces = jnp.zeros_like(load_blocks)
    for sweep_index in range(ITERS):
        coupled = load_blocks
        if sweep_index > 0:
            neighbours = lax.all_gather(traces[None], "row", axis=0, tiled=True)
            coupled = load_blocks + COUPLING * jnp.einsum(
                "n,nlo->lo", neighbour_weights, neighbours, precision=lax.Precision.HIGHEST
            )
        applied = lax.dot_general(
            coupled,
            flex_local,
            (((1,), (1,)), ((), ())),
            precision=lax.Precision.HIGHEST,
            preferred_element_type=jnp.float32,
        )
        traces = (1.0 - DAMPING) * traces + DAMPING * applied
    small = load_share // row_total
    rounded = traces.astype(jnp.bfloat16).reshape(row_total, small, order_rows)
    every_trace = lax.all_to_all(rounded, "row", split_axis=0, concat_axis=0, tiled=True)
    every_trace = every_trace.reshape(row_total, small, block_count, MBLK)
    every_trace = every_trace.transpose(1, 0, 2, 3).reshape(small, block_total, MBLK)
    updated = (
        jnp.take(every_trace, owner_map, axis=1) * pattern[None].astype(jnp.bfloat16)
    ).reshape(small, block_total * MBLK)
    all_loads = lax.all_gather(updated, "col", axis=0, tiled=True)

    def rows_of(source, index):
        return lax.dynamic_slice_in_dim(source, index * order_rows, order_rows, 1)

    other_a = lax.ppermute(rows_of(all_loads, own_row ^ 2), "row", across)
    other_b = lax.ppermute(rows_of(all_loads, own_row ^ 3), "row", across)
    mine = [rows_of(all_loads, own_row ^ k) for k in range(row_total)]

    gain = math.sqrt(column_count * col_total / (order_rows * row_total))
    width = column_count - gathered
    edges = [width * k // PIECES // TILE * TILE for k in range(PIECES)] + [width]
    arrivals = []
    for low, high in zip(edges[:-1], edges[1:]):
        start = gathered + low
        piece = product(
            [other_a, other_b],
            [panel, partner],
            gain,
            ([start, start], high - low),
            jax.ShapeDtypeStruct((group, high - low), jnp.bfloat16),
        )
        arrivals.append((start, high - low, lax.ppermute(piece, "row", across)))
    full = jax.ShapeDtypeStruct((group, column_count), jnp.float32)
    response = product(
        mine, [panel, partner, far, far_partner], gain, ([0] * 4, gathered), full
    )
    for start, size, arrived in arrivals:
        response = product(
            mine[:2], [panel, partner], gain, ([start, start], size), full, start, arrived, response
        )
    return response


def solution(mesh):
    in_specs = (P("row", "col"), P("col", None), P("row", None, None), P(), P("row", None), P())
    out_specs = P("row", "col")
    return jax.shard_map(body, mesh=mesh, in_specs=in_specs, out_specs=out_specs, check_vma=False)
```

```python
import functools
import math

import jax
import jax.numpy as jnp
from jax import lax
from jax.experimental import pallas as pl
from jax.experimental.pallas import tpu as pltpu
from jax.sharding import PartitionSpec as P

MBLK = 128
ITERS = 2
DAMPING = 0.6
COUPLING = 0.5
TILE = 512
GATHERED_SIXTEENTHS = 5
MESH = pl.DeviceIdType.MESH
PIECES = 3


def live_pattern(live_rows):
    offsets = jnp.arange(MBLK, dtype=jnp.int32)
    return (offsets[None, :] < live_rows[:, None]).astype(jnp.float32)


def product_kernel(count, gain, with_extra, with_base, *refs):
    factors, panels = refs[:count], refs[count : 2 * count]
    rest = refs[2 * count :]
    total = jnp.dot(factors[0][...], panels[0][...], preferred_element_type=jnp.float32)
    for factor, panel in zip(factors[1:], panels[1:]):
        total += jnp.dot(factor[...], panel[...], preferred_element_type=jnp.float32)
    total = gain * total
    if with_extra:
        total += rest[0][...].astype(jnp.float32)
    rest[-1][...] = total.astype(rest[-1].dtype)


def product(loads, depth, first, panels, gain, columns, out_shape, out_start=0, extra=None, base=None):
    starts, width = columns
    count = len(panels)
    rows = loads.shape[0]
    in_specs = [
        pl.BlockSpec((rows, depth), functools.partial(lambda k, j: (0, k), first + k))
        for k in range(count)
    ]
    for start in starts:
        in_specs.append(
            pl.BlockSpec((depth, TILE), functools.partial(lambda s, j: (0, s + j), start // TILE))
        )
    operands = [loads] * count + list(panels)
    if extra is not None:
        in_specs.append(pl.BlockSpec((rows, TILE), lambda j: (0, j)))
        operands.append(extra)
    aliases = {}
    if base is not None:
        in_specs.append(pl.BlockSpec(memory_space=pl.ANY))
        aliases = {len(operands): 0}
        operands.append(base)
    return pl.pallas_call(
        functools.partial(product_kernel, count, gain, extra is not None, base is not None),
        grid=(width // TILE,),
        in_specs=in_specs,
        out_specs=pl.BlockSpec(
            (rows, TILE), functools.partial(lambda s, j: (0, s + j), out_start // TILE)
        ),
        out_shape=out_shape,
        input_output_aliases=aliases,
        compiler_params=pltpu.CompilerParams(
            dimension_semantics=("arbitrary",), vmem_limit_bytes=40 * 1024 * 1024
        ),
        cost_estimate=pl.CostEstimate(
            flops=2 * rows * depth * count * width,
            bytes_accessed=2 * depth * count * width + 4 * rows * width,
            transcendentals=0,
        ),
    )(*operands)


def greet(axis, peers):
    barrier = pltpu.get_barrier_semaphore()
    for peer in peers:
        pl.semaphore_signal(barrier, inc=1, device_id={axis: peer}, device_id_type=MESH)
    pl.semaphore_wait(barrier, len(peers))


def send(axis, peer, source, target, send_sem, recv_sem):
    copy = pltpu.make_async_remote_copy(
        src_ref=source,
        dst_ref=target,
        send_sem=send_sem,
        recv_sem=recv_sem,
        device_id={axis: peer},
        device_id_type=MESH,
    )
    copy.start()
    return copy


def gather_kernel(axis, n, in_ref, out_ref, far_send, far_recv, near_send, near_recv):
    me = lax.axis_index(axis)
    inner, place, outer = me % 2, me // 2, n // 2
    partner = me + 1 - 2 * inner
    peers = [((place + k) % outer) * 2 + inner for k in range(1, outer)]
    greet(axis, [partner] + peers)
    far = []
    for k in range(1, outer):
        far.append(
            send(axis, peers[k - 1], in_ref, out_ref.at[me], far_send.at[k], far_recv.at[k])
        )
    near = [send(axis, partner, in_ref, out_ref.at[me], near_send.at[0], near_recv.at[0])]
    out_ref[me] = in_ref[...]
    for k in range(1, outer):
        source = ((place - k + outer) % outer) * 2 + inner
        far[k - 1].wait_recv()
        slot = out_ref.at[source]
        near.append(send(axis, partner, slot, slot, near_send.at[k], near_recv.at[k]))
    for copy in far:
        copy.wait_send()
    for copy in near:
        copy.wait()


def gather(block, axis, n, ident):
    return pl.pallas_call(
        functools.partial(gather_kernel, axis, n),
        out_shape=jax.ShapeDtypeStruct((n,) + block.shape, block.dtype),
        in_specs=[pl.BlockSpec(memory_space=pltpu.VMEM)],
        out_specs=pl.BlockSpec(memory_space=pltpu.VMEM),
        scratch_shapes=[pltpu.SemaphoreType.DMA((n // 2,))] * 4,
        compiler_params=pltpu.CompilerParams(collective_id=ident, has_side_effects=True),
    )(block)


def reduce_kernel(axis, n, part, out_ref, near_in, held, far_in, near_send, near_recv, far_send, far_recv):
    me = lax.axis_index(axis)
    inner, place, outer = me % 2, me // 2, n // 2
    partner = me + 1 - 2 * inner
    peers = [((place + k) % outer) * 2 + inner for k in range(outer)]
    greet(axis, [partner] + peers[1:])
    order = list(range(1, outer)) + [0]
    near = {}
    for k in order:
        near[k] = send(
            axis,
            partner,
            part.at[:, peers[k] + 1 - 2 * inner],
            near_in.at[k],
            near_send.at[k],
            near_recv.at[k],
        )
    far = {}
    for k in order[:-1]:
        near[k].wait_recv()
        held[k] = part[:, peers[k]] + near_in[k]
        far[k] = send(axis, peers[k], held.at[k], far_in.at[k], far_send.at[k], far_recv.at[k])
    near[0].wait_recv()
    out_ref[...] = part[:, me] + near_in[0]
    for k in order[:-1]:
        far[k].wait_recv()
        out_ref[...] += far_in[k]
    for k in order[:-1]:
        far[k].wait_send()
    for k in order:
        near[k].wait_send()


def reduce_scatter(partial, axis, n, ident):
    groups, _, rows, width = partial.shape
    block = (groups, rows, width)
    slots = pltpu.VMEM((n // 2,) + block, jnp.float32)
    return pl.pallas_call(
        functools.partial(reduce_kernel, axis, n),
        out_shape=jax.ShapeDtypeStruct(block, jnp.float32),
        in_specs=[pl.BlockSpec(memory_space=pltpu.VMEM)],
        out_specs=pl.BlockSpec(memory_space=pltpu.VMEM),
        scratch_shapes=[slots] * 3 + [pltpu.SemaphoreType.DMA((n // 2,))] * 4,
        compiler_params=pltpu.CompilerParams(collective_id=ident, has_side_effects=True),
    )(partial)


def swap_kernel(axis, in_ref, token_ref, out_ref, send_sem, recv_sem):
    del token_ref
    me = lax.axis_index(axis)
    partner = me + 1 - 2 * (me % 2)
    greet(axis, [partner])
    send(axis, partner, in_ref, out_ref, send_sem, recv_sem).wait()


def swap_after(array, token, axis, ident):
    return pl.pallas_call(
        functools.partial(swap_kernel, axis),
        out_shape=jax.ShapeDtypeStruct(array.shape, array.dtype),
        in_specs=[pl.BlockSpec(memory_space=pl.ANY)] * 2,
        out_specs=pl.BlockSpec(memory_space=pl.ANY),
        scratch_shapes=[pltpu.SemaphoreType.DMA] * 2,
        compiler_params=pltpu.CompilerParams(collective_id=ident, has_side_effects=True),
    )(array, token)


def body(panel, surface, flexibility, owner_map, adjacency, live_rows):
    order_rows, column_count = panel.shape
    row_total = lax.axis_size("row")
    col_total = lax.axis_size("col")
    own_row = lax.axis_index("row")
    load_total = surface.shape[1]
    load_share = load_total // col_total
    group = load_total // row_total
    small = group // col_total
    block_count = order_rows // MBLK
    block_total = owner_map.shape[0]
    swap = [(i, i ^ 1) for i in range(row_total)]
    across = [(i, i ^ 2) for i in range(row_total)]

    gathered = max(TILE, column_count * GATHERED_SIXTEENTHS // 16 // TILE * TILE)
    far = lax.ppermute(panel[:, :gathered], "row", across)
    partner = lax.ppermute(panel, "row", swap)

    partial = lax.dot_general(
        surface, panel, (((0,), (1,)), ((), ())), preferred_element_type=jnp.float32
    )
    traction = reduce_scatter(
        partial.reshape(row_total, col_total, small, order_rows), "col", col_total, 0
    ).reshape(load_share, order_rows)
    pattern = live_pattern(live_rows)
    own_pattern = lax.dynamic_slice_in_dim(pattern, own_row * block_count, block_count, 0)
    masked = traction * own_pattern.reshape(1, order_rows)
    every_block = gather(masked, "row", row_total, 1)
    every_block = every_block.reshape(row_total, load_share, block_count, MBLK)
    inverse = (
        jnp.zeros((block_total,), jnp.int32)
        .at[owner_map]
        .set(jnp.arange(block_total, dtype=jnp.int32))
    )
    own_sources = lax.dynamic_slice_in_dim(inverse, own_row * block_count, block_count, 0)
    every_block = every_block.transpose(0, 2, 1, 3).reshape(block_total, load_share, MBLK)
    load_blocks = jnp.take(every_block, own_sources, axis=0)
    load_blocks = load_blocks.transpose(1, 0, 2).reshape(load_share, order_rows)
    hits = adjacency[0][:, None] == jnp.arange(row_total, dtype=jnp.int32)[None, :]
    neighbour_weights = jnp.sum(hits.astype(jnp.float32), axis=0)
    flex_local = flexibility[0]
    traces = jnp.zeros_like(load_blocks)
    for sweep_index in range(ITERS):
        coupled = load_blocks
        if sweep_index > 0:
            neighbours = gather(traces, "row", row_total, 1 + sweep_index)
            coupled = load_blocks + COUPLING * jnp.sum(
                neighbour_weights[:, None, None] * neighbours, axis=0
            )
        applied = lax.dot_general(
            coupled,
            flex_local,
            (((1,), (1,)), ((), ())),
            precision=lax.Precision.HIGHEST,
            preferred_element_type=jnp.float32,
        )
        traces = (1.0 - DAMPING) * traces + DAMPING * applied
    every_trace = gather(traces.astype(jnp.bfloat16), "row", row_total, 1 + ITERS)
    every_trace = every_trace.reshape(row_total, row_total, small, block_count, MBLK)
    blocks = jnp.concatenate(
        [(own_row ^ k) * block_count + jnp.arange(block_count) for k in range(row_total)]
    )
    slots = jnp.take(owner_map, blocks)
    masks = jnp.take(pattern, blocks, axis=0).astype(jnp.bfloat16)

    def updated_for(load_group, count):
        mine = lax.dynamic_index_in_dim(every_trace, load_group, 1, keepdims=False)
        mine = mine.transpose(0, 2, 1, 3).reshape(block_total, small, MBLK)
        mine = jnp.take(mine, slots[:count], axis=0) * masks[:count, None, :]
        return mine.transpose(1, 0, 2).reshape(small, count * MBLK)

    wanted = jnp.concatenate(
        [updated_for(own_row, block_total), updated_for(own_row ^ 2, 2 * block_count)], axis=1
    )
    all_loads = gather(wanted, "col", col_total, 2 + ITERS).reshape(group, -1)

    gain = math.sqrt(column_count * col_total / (order_rows * row_total))
    width = column_count - gathered
    edges = [width * k // PIECES // TILE * TILE for k in range(PIECES)] + [width]
    arrivals = []
    for low, high in zip(edges[:-1], edges[1:]):
        start = gathered + low
        piece = product(
            all_loads,
            order_rows,
            row_total,
            [panel, partner],
            gain,
            ([start, start], high - low),
            jax.ShapeDtypeStruct((group, high - low), jnp.bfloat16),
        )
        arrivals.append((start, high - low, lax.ppermute(piece, "row", across)))
    far_partner = swap_after(far, piece, "row", 3 + ITERS)
    full = jax.ShapeDtypeStruct((group, column_count), jnp.float32)
    response = product(
        all_loads,
        order_rows,
        0,
        [panel, partner, far, far_partner],
        gain,
        ([0] * row_total, gathered),
        full,
    )
    for start, size, arrived in arrivals:
        response = product(
            all_loads,
            order_rows,
            0,
            [panel, partner],
            gain,
            ([start, start], size),
            full,
            start,
            arrived,
            response,
        )
    return response


def solution(mesh):
    in_specs = (P("row", "col"), P("col", None), P("row", None, None), P(), P("row", None), P())
    out_specs = P("row", "col")
    return jax.shard_map(body, mesh=mesh, in_specs=in_specs, out_specs=out_specs, check_vma=False)
```

```python
import functools
import math

import jax
import jax.numpy as jnp
from jax import lax
from jax.experimental import pallas as pl
from jax.experimental.pallas import tpu as pltpu
from jax.sharding import PartitionSpec as P


MBLK = 128
ITERS = 2
DAMPING = 0.6
COUPLING = 0.5
TILE = 512
EARLY_PART = 6
LATE_PART = 12
PARTS = 2
MESH = pl.DeviceIdType.MESH
PIECE_EDGES = (0, 2, 8, 14, 17, 18)


def live_pattern(live_rows):
    offsets = jnp.arange(MBLK, dtype=jnp.int32)
    return (offsets[None, :] < live_rows[:, None]).astype(jnp.float32)


def product_kernel(count, gain, with_extra, *refs):
    factors, panels = refs[:count], refs[count : 2 * count]
    rest = refs[2 * count :]
    total = jnp.dot(factors[0][...], panels[0][...], preferred_element_type=jnp.float32)
    for factor, panel in zip(factors[1:], panels[1:]):
        total += jnp.dot(factor[...], panel[...], preferred_element_type=jnp.float32)
    total = gain * total
    if with_extra:
        total += rest[0][...].astype(jnp.float32)
    rest[-1][...] = total.astype(rest[-1].dtype)


def product(loads, depth, first, panels, gain, columns, out_shape, out_start=0, extra=None, base=None, token=None):
    starts, width = columns
    count = len(panels)
    rows = loads.shape[0]
    in_specs = [
        pl.BlockSpec((rows, depth), functools.partial(lambda k, j: (0, k), first + k))
        for k in range(count)
    ]
    for start in starts:
        in_specs.append(
            pl.BlockSpec((depth, TILE), functools.partial(lambda s, j: (0, s + j), start // TILE))
        )
    operands = [loads] * count + list(panels)
    if extra is not None:
        in_specs.append(pl.BlockSpec((rows, TILE), lambda j: (0, j)))
        operands.append(extra)
    aliases = {}
    if token is not None:
        in_specs.append(pl.BlockSpec(memory_space=pl.ANY))
        operands.append(token)
    if base is not None:
        in_specs.append(pl.BlockSpec(memory_space=pl.ANY))
        aliases = {len(operands): 0}
        operands.append(base)
    return pl.pallas_call(
        functools.partial(product_kernel, count, gain, extra is not None),
        grid=(width // TILE,),
        in_specs=in_specs,
        out_specs=pl.BlockSpec(
            (rows, TILE), functools.partial(lambda s, j: (0, s + j), out_start // TILE)
        ),
        out_shape=out_shape,
        input_output_aliases=aliases,
        compiler_params=pltpu.CompilerParams(
            dimension_semantics=("arbitrary",), vmem_limit_bytes=40 * 1024 * 1024
        ),
        cost_estimate=pl.CostEstimate(
            flops=2 * rows * depth * count * width,
            bytes_accessed=2 * depth * count * width + 4 * rows * width,
            transcendentals=0,
        ),
    )(*operands)


def greet(axis, peers):
    barrier = pltpu.get_barrier_semaphore()
    for peer in peers:
        pl.semaphore_signal(barrier, inc=1, device_id={axis: peer}, device_id_type=MESH)
    pl.semaphore_wait(barrier, len(peers))


def send(axis, peer, source, target, send_sem, recv_sem):
    copy = pltpu.make_async_remote_copy(
        src_ref=source,
        dst_ref=target,
        send_sem=send_sem,
        recv_sem=recv_sem,
        device_id={axis: peer},
        device_id_type=MESH,
    )
    copy.start()
    return copy


def gather_kernel(axis, n, in_ref, out_ref, far_send, far_recv, near_send, near_recv):
    me = lax.axis_index(axis)
    inner, place, outer = me % 2, me // 2, n // 2
    partner = me + 1 - 2 * inner
    peers = [((place + k) % outer) * 2 + inner for k in range(1, outer)]
    greet(axis, [partner] + peers)
    width = in_ref.shape[-1] // PARTS
    spans = [pl.ds(part * width, width) for part in range(PARTS)]
    far, near = {}, []
    for part, span in enumerate(spans):
        near.append(
            send(
                axis,
                partner,
                in_ref.at[:, span],
                out_ref.at[me, :, span],
                near_send.at[0, part],
                near_recv.at[0, part],
            )
        )
        for k in range(1, outer):
            far[part, k] = send(
                axis,
                peers[k - 1],
                in_ref.at[:, span],
                out_ref.at[me, :, span],
                far_send.at[k, part],
                far_recv.at[k, part],
            )
    out_ref[me] = in_ref[...]
    for part, span in enumerate(spans):
        for k in range(1, outer):
            source = ((place - k + outer) % outer) * 2 + inner
            far[part, k].wait_recv()
            slot = out_ref.at[source, :, span]
            near.append(
                send(axis, partner, slot, slot, near_send.at[k, part], near_recv.at[k, part])
            )
    for copy in far.values():
        copy.wait_send()
    for copy in near:
        copy.wait()


def gather(block, axis, n, ident):
    return pl.pallas_call(
        functools.partial(gather_kernel, axis, n),
        out_shape=jax.ShapeDtypeStruct((n,) + block.shape, block.dtype),
        in_specs=[pl.BlockSpec(memory_space=pltpu.VMEM)],
        out_specs=pl.BlockSpec(memory_space=pltpu.VMEM),
        scratch_shapes=[pltpu.SemaphoreType.DMA((n // 2, PARTS))] * 4,
        compiler_params=pltpu.CompilerParams(collective_id=ident, has_side_effects=True),
    )(block)


def pick_kernel(sources, block_ref, out_ref):
    del sources
    out_ref[...] = block_ref[0]


def pick_blocks(every_block, sources):
    rows, width = every_block.shape[1:]
    per = width // MBLK
    return pl.pallas_call(
        pick_kernel,
        grid_spec=pltpu.PrefetchScalarGridSpec(
            num_scalar_prefetch=1,
            grid=(sources.shape[0],),
            in_specs=[
                pl.BlockSpec((1, rows, MBLK), lambda j, at: (at[j] // per, 0, at[j] % per))
            ],
            out_specs=pl.BlockSpec((rows, MBLK), lambda j, at: (0, j)),
        ),
        out_shape=jax.ShapeDtypeStruct((rows, sources.shape[0] * MBLK), every_block.dtype),
    )(sources, every_block)


def reduce_kernel(axis, n, part, out_ref, near_in, held, far_in, near_send, near_recv, far_send, far_recv):
    me = lax.axis_index(axis)
    inner, place, outer = me % 2, me // 2, n // 2
    partner = me + 1 - 2 * inner
    peers = [((place + k) % outer) * 2 + inner for k in range(outer)]
    greet(axis, [partner] + peers[1:])
    order = list(range(1, outer)) + [0]
    near = {}
    for k in order:
        near[k] = send(
            axis,
            partner,
            part.at[:, peers[k] + 1 - 2 * inner],
            near_in.at[k],
            near_send.at[k],
            near_recv.at[k],
        )
    far = {}
    for k in order[:-1]:
        near[k].wait_recv()
        held[k] = part[:, peers[k]] + near_in[k]
        far[k] = send(axis, peers[k], held.at[k], far_in.at[k], far_send.at[k], far_recv.at[k])
    near[0].wait_recv()
    out_ref[...] = part[:, me] + near_in[0]
    for k in order[:-1]:
        far[k].wait_recv()
        out_ref[...] += far_in[k]
    for k in order[:-1]:
        far[k].wait_send()
    for k in order:
        near[k].wait_send()


def reduce_scatter(partial, axis, n, ident):
    groups, _, rows, width = partial.shape
    block = (groups, rows, width)
    slots = pltpu.VMEM((n // 2,) + block, jnp.float32)
    return pl.pallas_call(
        functools.partial(reduce_kernel, axis, n),
        out_shape=jax.ShapeDtypeStruct(block, jnp.float32),
        in_specs=[pl.BlockSpec(memory_space=pltpu.VMEM)],
        out_specs=pl.BlockSpec(memory_space=pltpu.VMEM),
        scratch_shapes=[slots] * 3 + [pltpu.SemaphoreType.DMA((n // 2,))] * 4,
        compiler_params=pltpu.CompilerParams(collective_id=ident, has_side_effects=True),
    )(partial)


def swap_kernel(axis, first_ref, second_ref, token_ref, first_out, second_out, send_sem, recv_sem):
    del token_ref
    me = lax.axis_index(axis)
    partner = me + 1 - 2 * (me % 2)
    greet(axis, [partner])
    first = send(axis, partner, first_ref, first_out, send_sem.at[0], recv_sem.at[0])
    second = send(axis, partner, second_ref, second_out, send_sem.at[1], recv_sem.at[1])
    first.wait()
    second.wait()


def swap_after(arrays, token, axis, ident):
    return pl.pallas_call(
        functools.partial(swap_kernel, axis),
        out_shape=[jax.ShapeDtypeStruct(array.shape, array.dtype) for array in arrays],
        in_specs=[pl.BlockSpec(memory_space=pl.ANY)] * 3,
        out_specs=[pl.BlockSpec(memory_space=pl.ANY)] * 2,
        scratch_shapes=[pltpu.SemaphoreType.DMA((2,))] * 2,
        compiler_params=pltpu.CompilerParams(collective_id=ident, has_side_effects=True),
    )(*arrays, token)


def steps(panel, surface, flexibility, owner_map, adjacency, live_rows):
    order_rows, column_count = panel.shape
    row_total = lax.axis_size("row")
    col_total = lax.axis_size("col")
    own_row = lax.axis_index("row")
    load_total = surface.shape[1]
    load_share = load_total // col_total
    group = load_total // row_total
    small = group // col_total
    block_count = order_rows // MBLK
    block_total = owner_map.shape[0]
    swap = [(i, i ^ 1) for i in range(row_total)]
    across = [(i, i ^ 2) for i in range(row_total)]

    early = max(TILE, column_count // EARLY_PART // TILE * TILE)
    late = max(TILE, column_count // LATE_PART // TILE * TILE)
    gathered = early + late
    far = lax.ppermute(panel[:, :early], "row", across)
    partner = lax.ppermute(panel, "row", swap)

    partial = lax.dot_general(
        surface, panel, (((0,), (1,)), ((), ())), preferred_element_type=jnp.float32
    )
    traction = reduce_scatter(
        partial.reshape(row_total, col_total, small, order_rows), "col", col_total, 0
    ).reshape(load_share, order_rows)
    pattern = live_pattern(live_rows)
    own_pattern = lax.dynamic_slice_in_dim(pattern, own_row * block_count, block_count, 0)
    masked = traction * own_pattern.reshape(1, order_rows)
    every_block = gather(masked, "row", row_total, 1)
    inverse = (
        jnp.zeros((block_total,), jnp.int32)
        .at[owner_map]
        .set(jnp.arange(block_total, dtype=jnp.int32))
    )
    own_sources = lax.dynamic_slice_in_dim(inverse, own_row * block_count, block_count, 0)
    load_blocks = pick_blocks(every_block, own_sources)
    hits = adjacency[0][:, None] == jnp.arange(row_total, dtype=jnp.int32)[None, :]
    neighbour_weights = jnp.sum(hits.astype(jnp.float32), axis=0)
    flex_local = flexibility[0]
    traces = jnp.zeros_like(load_blocks)
    for sweep_index in range(ITERS):
        coupled = load_blocks
        if sweep_index > 0:
            neighbours = gather(traces, "row", row_total, 1 + sweep_index)
            coupled = load_blocks + COUPLING * jnp.sum(
                neighbour_weights[:, None, None] * neighbours, axis=0
            )
        applied = lax.dot_general(
            coupled,
            flex_local,
            (((1,), (1,)), ((), ())),
            precision=lax.Precision.HIGHEST,
            preferred_element_type=jnp.float32,
        )
        traces = (1.0 - DAMPING) * traces + DAMPING * applied
    every_trace = gather(traces.astype(jnp.bfloat16), "row", row_total, 1 + ITERS)
    late_panel, every_trace = lax.optimization_barrier(
        (panel[:, early:gathered], every_trace)
    )
    far_late = lax.ppermute(late_panel, "row", across)
    every_trace = every_trace.reshape(row_total, row_total, small, block_count, MBLK)
    blocks = jnp.concatenate(
        [(own_row ^ k) * block_count + jnp.arange(block_count) for k in range(row_total)]
    )
    slots = jnp.take(owner_map, blocks)
    masks = jnp.take(pattern, blocks, axis=0).astype(jnp.bfloat16)

    def updated_for(load_group, count):
        mine = lax.dynamic_index_in_dim(every_trace, load_group, 1, keepdims=False)
        mine = mine.transpose(0, 2, 1, 3).reshape(block_total, small, MBLK)
        mine = jnp.take(mine, slots[:count], axis=0) * masks[:count, None, :]
        return mine.transpose(1, 0, 2).reshape(small, count * MBLK)

    wanted = jnp.concatenate(
        [updated_for(own_row, block_total), updated_for(own_row ^ 2, 2 * block_count)], axis=1
    )
    all_loads = gather(wanted, "col", col_total, 2 + ITERS).reshape(group, -1)

    gain = math.sqrt(column_count * col_total / (order_rows * row_total))
    width = column_count - gathered
    tiles = width // TILE
    edges = sorted({tiles * edge // PIECE_EDGES[-1] * TILE for edge in PIECE_EDGES})
    arrivals, piece = [], None
    for low, high in zip(edges[:-1], edges[1:]):
        start = gathered + low
        piece = product(
            all_loads,
            order_rows,
            row_total,
            [panel, partner],
            gain,
            ([start, start], high - low),
            jax.ShapeDtypeStruct((group, high - low), jnp.bfloat16),
            token=piece,
        )
        arrivals.append((start, high - low, lax.ppermute(piece, "row", across)))
    far_partner, late_partner = swap_after([far, far_late], piece, "row", 3 + ITERS)
    full = jax.ShapeDtypeStruct((group, column_count), jnp.float32)
    response = product(
        all_loads,
        order_rows,
        0,
        [panel, partner, far, far_partner],
        gain,
        ([0] * row_total, early),
        full,
    )
    response = product(
        all_loads,
        order_rows,
        0,
        [panel, partner, far_late, late_partner],
        gain,
        ([early, early, 0, 0], late),
        full,
        early,
        None,
        response,
    )
    for start, size, arrived in arrivals:
        response = product(
            all_loads,
            order_rows,
            0,
            [panel, partner],
            gain,
            ([start, start], size),
            full,
            start,
            arrived,
            response,
        )
    return response


def solution(mesh):
    in_specs = (P("row", "col"), P("col", None), P("row", None, None), P(), P("row", None), P())
    out_specs = P("row", "col")
    return jax.shard_map(steps, mesh=mesh, in_specs=in_specs, out_specs=out_specs, check_vma=False)
```

```python
import functools
import math

import jax
import jax.numpy as jnp
from jax import lax
from jax.experimental import pallas as pl
from jax.experimental.pallas import tpu as pltpu
from jax.sharding import PartitionSpec as P


MBLK = 128
ITERS = 2
DAMPING = 0.6
COUPLING = 0.5
TILE = 512
EARLY_PART = 5
LATE_PART = 2
WHOLE_PART = 24
PARTS = 3
HALVES = 2
MESH = pl.DeviceIdType.MESH
PIECE_EDGES = (0, 2, 8, 14, 17, 18)


def live_pattern(live_rows):
    offsets = jnp.arange(MBLK, dtype=jnp.int32)
    return (offsets[None, :] < live_rows[:, None]).astype(jnp.float32)


def product_kernel(count, gain, with_extra, *refs):
    factors, panels = refs[:count], refs[count : 2 * count]
    rest = refs[2 * count :]
    total = jnp.dot(factors[0][...], panels[0][...], preferred_element_type=jnp.float32)
    for factor, panel in zip(factors[1:], panels[1:]):
        total += jnp.dot(factor[...], panel[...], preferred_element_type=jnp.float32)
    total = gain * total
    if with_extra:
        total += rest[0][...].astype(jnp.float32)
    rest[-1][...] = total.astype(rest[-1].dtype)


def product(loads, depth, first, panels, gain, columns, out_shape, out_start=0, extra=None, base=None, token=None):
    starts, width = columns
    count = len(panels)
    rows = loads.shape[0]
    in_specs = [
        pl.BlockSpec((rows, depth), functools.partial(lambda k, j: (0, k), first + k))
        for k in range(count)
    ]
    for start in starts:
        in_specs.append(
            pl.BlockSpec((depth, TILE), functools.partial(lambda s, j: (0, s + j), start // TILE))
        )
    operands = [loads] * count + list(panels)
    if extra is not None:
        in_specs.append(pl.BlockSpec((rows, TILE), lambda j: (0, j)))
        operands.append(extra)
    aliases = {}
    if token is not None:
        in_specs.append(pl.BlockSpec(memory_space=pl.ANY))
        operands.append(token)
    if base is not None:
        in_specs.append(pl.BlockSpec(memory_space=pl.ANY))
        aliases = {len(operands): 0}
        operands.append(base)
    return pl.pallas_call(
        functools.partial(product_kernel, count, gain, extra is not None),
        grid=(width // TILE,),
        in_specs=in_specs,
        out_specs=pl.BlockSpec(
            (rows, TILE), functools.partial(lambda s, j: (0, s + j), out_start // TILE)
        ),
        out_shape=out_shape,
        input_output_aliases=aliases,
        compiler_params=pltpu.CompilerParams(
            dimension_semantics=("arbitrary",), vmem_limit_bytes=40 * 1024 * 1024
        ),
        cost_estimate=pl.CostEstimate(
            flops=2 * rows * depth * count * width,
            bytes_accessed=2 * depth * count * width + 4 * rows * width,
            transcendentals=0,
        ),
    )(*operands)


def greet(axis, peers):
    barrier = pltpu.get_barrier_semaphore()
    for peer in peers:
        pl.semaphore_signal(barrier, inc=1, device_id={axis: peer}, device_id_type=MESH)
    pl.semaphore_wait(barrier, len(peers))


def send(axis, peer, source, target, send_sem, recv_sem):
    copy = pltpu.make_async_remote_copy(
        src_ref=source,
        dst_ref=target,
        send_sem=send_sem,
        recv_sem=recv_sem,
        device_id={axis: peer},
        device_id_type=MESH,
    )
    copy.start()
    return copy


def gather_kernel(axis, n, in_ref, out_ref, far_send, far_recv, near_send, near_recv):
    me = lax.axis_index(axis)
    inner, place, outer = me % 2, me // 2, n // 2
    partner = me + 1 - 2 * inner
    peers = [((place + k) % outer) * 2 + inner for k in range(1, outer)]
    greet(axis, [partner] + peers)
    width = in_ref.shape[-1] // PARTS
    spans = [pl.ds(part * width, width) for part in range(PARTS)]
    far, near = {}, []
    for part, span in enumerate(spans):
        near.append(
            send(
                axis,
                partner,
                in_ref.at[:, span],
                out_ref.at[me, :, span],
                near_send.at[0, part],
                near_recv.at[0, part],
            )
        )
        for k in range(1, outer):
            far[part, k] = send(
                axis,
                peers[k - 1],
                in_ref.at[:, span],
                out_ref.at[me, :, span],
                far_send.at[k, part],
                far_recv.at[k, part],
            )
    out_ref[me] = in_ref[...]
    for part, span in enumerate(spans):
        for k in range(1, outer):
            source = ((place - k + outer) % outer) * 2 + inner
            far[part, k].wait_recv()
            slot = out_ref.at[source, :, span]
            near.append(
                send(axis, partner, slot, slot, near_send.at[k, part], near_recv.at[k, part])
            )
    for copy in far.values():
        copy.wait_send()
    for copy in near:
        copy.wait()


def gather(block, axis, n, ident):
    return pl.pallas_call(
        functools.partial(gather_kernel, axis, n),
        out_shape=jax.ShapeDtypeStruct((n,) + block.shape, block.dtype),
        in_specs=[pl.BlockSpec(memory_space=pltpu.VMEM)],
        out_specs=pl.BlockSpec(memory_space=pltpu.VMEM),
        scratch_shapes=[pltpu.SemaphoreType.DMA((n // 2, PARTS))] * 4,
        compiler_params=pltpu.CompilerParams(collective_id=ident, has_side_effects=True),
    )(block)


def pick_kernel(sources, block_ref, out_ref):
    del sources
    out_ref[...] = block_ref[0]


def pick_blocks(every_block, sources):
    rows, width = every_block.shape[1:]
    per = width // MBLK
    return pl.pallas_call(
        pick_kernel,
        grid_spec=pltpu.PrefetchScalarGridSpec(
            num_scalar_prefetch=1,
            grid=(sources.shape[0],),
            in_specs=[
                pl.BlockSpec((1, rows, MBLK), lambda j, at: (at[j] // per, 0, at[j] % per))
            ],
            out_specs=pl.BlockSpec((rows, MBLK), lambda j, at: (0, j)),
        ),
        out_shape=jax.ShapeDtypeStruct((rows, sources.shape[0] * MBLK), every_block.dtype),
    )(sources, every_block)


def reduce_kernel(axis, n, part, out_ref, near_in, held, far_in, near_send, near_recv, far_send, far_recv):
    me = lax.axis_index(axis)
    inner, place, outer = me % 2, me // 2, n // 2
    partner = me + 1 - 2 * inner
    peers = [((place + k) % outer) * 2 + inner for k in range(outer)]
    greet(axis, [partner] + peers[1:])
    depth = part.shape[0] // HALVES
    order = [(k, h) for k in list(range(1, outer)) + [0] for h in range(HALVES)]
    spans = [pl.ds(h * depth, depth) for h in range(HALVES)]
    near = {}
    for k, h in order:
        near[k, h] = send(
            axis,
            partner,
            part.at[spans[h], peers[k] + 1 - 2 * inner],
            near_in.at[k, spans[h]],
            near_send.at[k, h],
            near_recv.at[k, h],
        )
    far = {}
    for k, h in order:
        near[k, h].wait_recv()
        span = spans[h]
        if k == 0:
            out_ref[span] = part[span, me] + near_in[0, span]
            continue
        held[k, span] = part[span, peers[k]] + near_in[k, span]
        far[k, h] = send(
            axis,
            peers[k],
            held.at[k, span],
            far_in.at[k, span],
            far_send.at[k, h],
            far_recv.at[k, h],
        )
    for k, h in far:
        far[k, h].wait_recv()
        out_ref[spans[h]] += far_in[k, spans[h]]
    for copy in far.values():
        copy.wait_send()
    for copy in near.values():
        copy.wait_send()


def reduce_scatter(partial, axis, n, ident):
    groups, _, rows, width = partial.shape
    block = (groups, rows, width)
    slots = pltpu.VMEM((n // 2,) + block, jnp.float32)
    return pl.pallas_call(
        functools.partial(reduce_kernel, axis, n),
        out_shape=jax.ShapeDtypeStruct(block, jnp.float32),
        in_specs=[pl.BlockSpec(memory_space=pltpu.VMEM)],
        out_specs=pl.BlockSpec(memory_space=pltpu.VMEM),
        scratch_shapes=[slots] * 3 + [pltpu.SemaphoreType.DMA((n // 2, HALVES))] * 4,
        compiler_params=pltpu.CompilerParams(collective_id=ident, has_side_effects=True),
    )(partial)


def swap_kernel(axis, first_ref, second_ref, token_ref, first_out, second_out, send_sem, recv_sem):
    del token_ref
    me = lax.axis_index(axis)
    partner = me + 1 - 2 * (me % 2)
    greet(axis, [partner])
    first = send(axis, partner, first_ref, first_out, send_sem.at[0], recv_sem.at[0])
    second = send(axis, partner, second_ref, second_out, send_sem.at[1], recv_sem.at[1])
    first.wait()
    second.wait()


def swap_after(arrays, token, axis, ident):
    return pl.pallas_call(
        functools.partial(swap_kernel, axis),
        out_shape=[jax.ShapeDtypeStruct(array.shape, array.dtype) for array in arrays],
        in_specs=[pl.BlockSpec(memory_space=pl.ANY)] * 3,
        out_specs=[pl.BlockSpec(memory_space=pl.ANY)] * 2,
        scratch_shapes=[pltpu.SemaphoreType.DMA((2,))] * 2,
        compiler_params=pltpu.CompilerParams(collective_id=ident, has_side_effects=True),
    )(*arrays, token)


def steps(panel, surface, flexibility, owner_map, adjacency, live_rows):
    order_rows, column_count = panel.shape
    row_total = lax.axis_size("row")
    col_total = lax.axis_size("col")
    own_row = lax.axis_index("row")
    load_total = surface.shape[1]
    load_share = load_total // col_total
    group = load_total // row_total
    small = group // col_total
    block_count = order_rows // MBLK
    block_total = owner_map.shape[0]
    swap = [(i, i ^ 1) for i in range(row_total)]
    across = [(i, i ^ 2) for i in range(row_total)]

    early = max(TILE, column_count * EARLY_PART // WHOLE_PART // TILE * TILE)
    late = max(TILE, column_count * LATE_PART // WHOLE_PART // TILE * TILE)
    gathered = early + late
    far = lax.ppermute(panel[:, :early], "row", across)
    partner = lax.ppermute(panel, "row", swap)

    partial = lax.dot_general(
        surface, panel, (((0,), (1,)), ((), ())), preferred_element_type=jnp.float32
    )
    traction = reduce_scatter(
        partial.reshape(row_total, col_total, small, order_rows), "col", col_total, 0
    ).reshape(load_share, order_rows)
    pattern = live_pattern(live_rows)
    own_pattern = lax.dynamic_slice_in_dim(pattern, own_row * block_count, block_count, 0)
    masked = traction * own_pattern.reshape(1, order_rows)
    every_block = gather(masked, "row", row_total, 1)
    inverse = (
        jnp.zeros((block_total,), jnp.int32)
        .at[owner_map]
        .set(jnp.arange(block_total, dtype=jnp.int32))
    )
    own_sources = lax.dynamic_slice_in_dim(inverse, own_row * block_count, block_count, 0)
    load_blocks = pick_blocks(every_block, own_sources)
    hits = adjacency[0][:, None] == jnp.arange(row_total, dtype=jnp.int32)[None, :]
    neighbour_weights = jnp.sum(hits.astype(jnp.float32), axis=0)
    flex_local = flexibility[0]
    traces = jnp.zeros_like(load_blocks)
    for sweep_index in range(ITERS):
        coupled = load_blocks
        if sweep_index > 0:
            neighbours = gather(traces, "row", row_total, 1 + sweep_index)
            coupled = load_blocks + COUPLING * jnp.sum(
                neighbour_weights[:, None, None] * neighbours, axis=0
            )
        applied = lax.dot_general(
            coupled,
            flex_local,
            (((1,), (1,)), ((), ())),
            precision=lax.Precision.HIGHEST,
            preferred_element_type=jnp.float32,
        )
        traces = (1.0 - DAMPING) * traces + DAMPING * applied
    every_trace = gather(traces.astype(jnp.bfloat16), "row", row_total, 1 + ITERS)
    late_panel, every_trace = lax.optimization_barrier(
        (panel[:, early:gathered], every_trace)
    )
    far_late = lax.ppermute(late_panel, "row", across)
    every_trace = every_trace.reshape(row_total, row_total, small, block_count, MBLK)
    blocks = jnp.concatenate(
        [(own_row ^ k) * block_count + jnp.arange(block_count) for k in range(row_total)]
    )
    slots = jnp.take(owner_map, blocks)
    masks = jnp.take(pattern, blocks, axis=0).astype(jnp.bfloat16)

    def updated_for(load_group, count):
        mine = lax.dynamic_index_in_dim(every_trace, load_group, 1, keepdims=False)
        mine = mine.transpose(0, 2, 1, 3).reshape(block_total, small, MBLK)
        mine = jnp.take(mine, slots[:count], axis=0) * masks[:count, None, :]
        return mine.transpose(1, 0, 2).reshape(small, count * MBLK)

    wanted = jnp.concatenate(
        [updated_for(own_row, block_total), updated_for(own_row ^ 2, 2 * block_count)], axis=1
    )
    all_loads = gather(wanted, "col", col_total, 2 + ITERS).reshape(group, -1)

    gain = math.sqrt(column_count * col_total / (order_rows * row_total))
    width = column_count - gathered
    tiles = width // TILE
    edges = sorted({tiles * edge // PIECE_EDGES[-1] * TILE for edge in PIECE_EDGES})
    arrivals, piece = [], None
    for low, high in zip(edges[:-1], edges[1:]):
        start = gathered + low
        piece = product(
            all_loads,
            order_rows,
            row_total,
            [panel, partner],
            gain,
            ([start, start], high - low),
            jax.ShapeDtypeStruct((group, high - low), jnp.bfloat16),
            token=piece,
        )
        arrivals.append((start, high - low, lax.ppermute(piece, "row", across)))
    far_partner, late_partner = swap_after([far, far_late], piece, "row", 3 + ITERS)
    full = jax.ShapeDtypeStruct((group, column_count), jnp.float32)
    response = product(
        all_loads,
        order_rows,
        0,
        [panel, partner, far, far_partner],
        gain,
        ([0] * row_total, early),
        full,
    )
    response = product(
        all_loads,
        order_rows,
        0,
        [panel, partner, far_late, late_partner],
        gain,
        ([early, early, 0, 0], late),
        full,
        early,
        None,
        response,
    )
    for start, size, arrived in arrivals:
        response = product(
            all_loads,
            order_rows,
            0,
            [panel, partner],
            gain,
            ([start, start], size),
            full,
            start,
            arrived,
            response,
        )
    return response


def solution(mesh):
    in_specs = (P("row", "col"), P("col", None), P("row", None, None), P(), P("row", None), P())
    out_specs = P("row", "col")
    return jax.shard_map(steps, mesh=mesh, in_specs=in_specs, out_specs=out_specs, check_vma=False)
```
